32 devices in a mesh: row: 4 (over y, core), col: 8 (over z, x).
Axes of the slice: x: 2, y: 2, z: 4, core: 2. Of those that a mesh axis runs over, the one named last changes fastest.
Arguments:
- integrals: bfloat16 [4, 8, 32, 512, 512], P('row', 'col'), may hold values from -0.0625 to 0.0625
- tile_count: int32 [4, 8], P('row', 'col'), may hold values from 1 to 32, as said below
- tile_list: int32 [4, 8, 32], P('row', 'col'), may hold values from 0 to 31, as said below
- amplitudes: bfloat16 [32, 512, 1024], P('col', 'row'), may hold values from -6 to 6
- pair_energy: float32 [16384], P(('row', 'col')), may hold values from 1 to 4
- occ_energy: float32 [32], replicated, may hold values from -1.5 to -0.25
- partner: int32 [16384], P(('row', 'col')), may hold values from 0 to 16383, as said below
Outputs:
- amp_update: float32 [16384, 1024], P(('row', 'col'))
The draws below stay inside these ranges and needn't reach their ends.
Inputs may be any that keep to these rules, and one draw needn't show every extreme that they name: `tile_count`: some grid cell holds exactly 32 live tiles. `tile_list`: each grid cell's list is a permutation of 0 to 31; only its first tile_count entries name live tiles. partner is an involution. Numbering the rows in consecutive blocks of 512, the rows of one block have their partners among the 8 blocks of the same aligned group of 4096 rows, exactly 64 of them in each of these blocks.
All inputs are finite; a program needn't handle non-finite values.
Results may differ from the reference program's by a relative error of at most 0.0003.
Values may be sent and summed in bfloat16 or wider, within the bound.
A program may use at most 128 MiB of HBM per device.

```python
import math
import jax
import jax.numpy as jnp
from jax import lax

TILE = 512
NO = 32
BC = 4
OCC = 1024
NBLK = 32
BR = 8
CAP = 32
NPAIRS = 16384
ROWS = 512
PEER = 64
N_ROW = 4
N_COL = 8


def shuffle_cap(subkey):
    return jax.random.permutation(subkey, CAP).astype(jnp.int32)


def shuffle_rows(subkey):
    return jax.random.permutation(subkey, ROWS).astype(jnp.int32)


def draw_tile_count(key, part):
    counts = jax.random.randint(key, (N_ROW * N_COL,), 1, CAP + 1).astype(jnp.int32)
    chosen = jax.random.randint(jax.random.fold_in(key, 7), (), 0, N_ROW * N_COL)
    counts = jnp.where(jnp.arange(N_ROW * N_COL) == chosen, CAP, counts)
    return counts.reshape(N_ROW, N_COL).astype(jnp.int32)


def draw_tile_list(key, part):
    subkeys = jax.random.split(jax.random.fold_in(key, 11), N_ROW * N_COL)
    orders = jax.vmap(shuffle_cap)(subkeys)
    return orders.reshape(N_ROW, N_COL, CAP).astype(jnp.int32)


def draw_partner(key, part):
    subkeys = jax.random.split(jax.random.fold_in(key, 13), N_ROW * N_COL)
    orders = jax.vmap(shuffle_rows)(subkeys).reshape(N_ROW, N_COL, ROWS)
    inverse = jnp.argsort(orders, axis=2).astype(jnp.int32)
    target = inverse // PEER
    within = inverse % PEER
    grid_row = jnp.arange(N_ROW, dtype=jnp.int32)[:, None, None]
    grid_col = jnp.arange(N_COL, dtype=jnp.int32)[None, :, None]
    local_row = orders[grid_row, target, grid_col * PEER + within]
    result = (grid_row * N_COL + target) * ROWS + local_row
    return result.reshape(N_ROW * N_COL * ROWS).astype(jnp.int32)


def block_levels(stream_key, dims, cuts, least, largest):
    gain, own = 1.0, jax.random.fold_in(stream_key, 6)
    for axis_at, blocks in cuts:
        draws = jnp.exp(jax.random.uniform(jax.random.fold_in(own, axis_at), (blocks,), jnp.float32, least / len(cuts), largest / len(cuts)))
        gain = gain * jnp.repeat(draws, dims[axis_at] // blocks).reshape([-1 if axis == axis_at else 1 for axis in range(len(dims))])
    return gain


def noise(rng, dims, spread, most, cuts=(), held_as=jnp.bfloat16):
    drawn = spread * jax.random.normal(rng, dims, jnp.float32)
    if cuts:
        drawn = drawn * block_levels(rng, dims, cuts, -0.22, 0.18)
    return jnp.clip(drawn, -most, most).astype(held_as)


def setup_inputs(seed: int = 0) -> dict:
    key_list = jax.random.split(jax.random.key(seed), 8)
    return {
        "integrals": noise(key_list[0], (N_ROW, N_COL, CAP, TILE, TILE), (NBLK * TILE // 2) ** -0.5, 0.0625, ((0, 4), (1, 8))),
        "tile_count": draw_tile_count(jax.random.fold_in(key_list[7], 71), 0),
        "tile_list": draw_tile_list(jax.random.fold_in(key_list[7], 71), 0),
        "amplitudes": noise(key_list[3], (NBLK, TILE, OCC), 1.0, 6.0, ((0, 8), (1, 4))),
        "pair_energy": jnp.clip(jnp.exp(math.log(4.0) - 1.3862944 * jax.random.uniform(key_list[4], (NPAIRS,), jnp.float32) ** block_levels(key_list[4], (NPAIRS,), ((0, 32),), -0.2, 0.2)), 1.0, 4.0),
        "occ_energy": jnp.clip(jax.random.uniform(key_list[5], (NO,), jnp.float32, -1.5, -0.25), -1.5, -0.25),
        "partner": draw_partner(jax.random.fold_in(key_list[7], 71), 0),
    }


def reference(integrals, tile_count, tile_list, amplitudes, pair_energy, occ_energy, partner):
    residual = jnp.zeros((NBLK, TILE, OCC), jnp.float32)

    def per_device(device, running):
        grid_row = (device // N_COL).astype(jnp.int32)
        grid_col = (device % N_COL).astype(jnp.int32)
        count_here = tile_count[grid_row, grid_col]

        def per_slot(slot, inner):
            position = tile_list[grid_row, grid_col, slot]
            block_row = grid_row * BR + position // BC
            block_col = grid_col * BC + position % BC
            product = jnp.dot(integrals[grid_row, grid_col, slot], amplitudes[block_col], preferred_element_type=jnp.float32)
            current = lax.dynamic_index_in_dim(inner, block_row, 0, keepdims=False)
            return lax.dynamic_update_index_in_dim(inner, current + product, block_row, 0)

        return lax.fori_loop(0, count_here, per_slot, running)

    residual = lax.fori_loop(0, N_ROW * N_COL, per_device, residual)
    flat_rows = residual.reshape(NPAIRS, OCC)
    mirrored = jnp.take(flat_rows, partner, axis=0).reshape(NPAIRS, NO, NO)
    mirrored = jnp.swapaxes(mirrored, 1, 2).reshape(NPAIRS, OCC)
    denominator = pair_energy[:, None] - (occ_energy[:, None] + occ_energy[None, :]).reshape(1, OCC)
    return (flat_rows + mirrored) / denominator
```

```python
import functools

import jax
import jax.numpy as jnp
from jax import lax
from jax.experimental import pallas as pl
from jax.experimental.pallas import tpu as pltpu
from jax.sharding import PartitionSpec as P

MESH = pl.DeviceIdType.MESH
F32, BF16, I32, I16 = jnp.float32, jnp.bfloat16, jnp.int32, jnp.int16
LEVELS = 32767.0
PIECE = 32
WIDE = 256


def iota(shape, axis):
    return lax.broadcasted_iota(I32, shape, axis)


def one_hot_of(condition):
    return condition.astype(F32).astype(BF16)


def dot(a, b):
    return jnp.dot(a, b, preferred_element_type=F32)


def dot_nt(a, b):
    return lax.dot_general(a, b, (((1,), (1,)), ((), ())), preferred_element_type=F32)


def ladder_kernel(
    n, ranks, occ, list_ref, count_ref, partner_ref, integrals, amps, out_ref,
    tiles, amp, tall, t2, u_ref, w_ref, hot_s, places, slot_s, q, mix, sbuf, z, hot, stack,
    q1s, s1s, q1r, s1r, q2s, s2s, q2r, s2r, q3s, s3s, q3r, s3r, xqs, xss, xqr, xsr,
    tile_sem, amp_sem, tsend, trecv, gsend, grecv,
    q1a, q1b, s1a, s1b, q2a, q2b, s2a, s2b, q3a, q3b, s3a, s3b, xqa, xqb, xsa, xsb,
):
    me = lax.axis_index("col")
    row = lax.axis_index("row")
    mate = row + 1 - 2 * lax.rem(row, 2)
    slots = list_ref.shape[0]
    rows = partner_ref.shape[1]
    half = rows // n // 2
    own = (n + 1) * half
    own_p = u_ref.shape[1]
    parts, bc, tile, wide = tall.shape
    depth = bc * tile
    share = amp.shape[1]
    width = amp.shape[2]
    groups = slots // 4
    m = n // 4
    hops = range(2, ranks, 2)

    def load_tiles(g):
        at = pl.ds(g * groups, groups)
        return pltpu.make_async_copy(integrals.at[0, 0, at], tiles.at[at], tile_sem.at[g])

    load_amp = pltpu.make_async_copy(amps, amp, amp_sem)
    load_amp.start()
    for g in range(4):
        load_tiles(g).start()

    barrier = pltpu.get_barrier_semaphore()
    for d in range(1, n):
        pl.semaphore_signal(barrier, inc=1, device_id={"col": lax.rem(me + d, n)}, device_id_type=MESH)
    pl.semaphore_signal(barrier, inc=1, device_id={"row": mate}, device_id_type=MESH)
    for k in hops:
        pl.semaphore_signal(barrier, inc=1, device_id={"row": lax.rem(row + k, ranks)}, device_id_type=MESH)

    def order(turn):
        return jnp.where(turn == 0, 0, jnp.where(turn == 1, parts - 1, turn - 1))

    @pl.loop(0, parts)
    def _(c):
        number = iota((width, wide), 1) + c * wide
        i = number & (occ - 1)
        s = number // occ
        q[c] = one_hot_of(iota((width, wide), 0) == i * occ + ((s - i) & (occ - 1)))
        number = iota((wide, wide), 1)
        i = number & (occ - 1)
        s = number // occ + c * (wide // occ)
        mix[c] = one_hot_of(iota((wide, wide), 0) == number - i + ((s - i) & (occ - 1)))

    def piece(c, source):
        return tall.at[c, :, pl.ds(pl.multiple_of(source * share, share), share), :]

    load_amp.wait()

    @pl.loop(0, parts)
    def _(c):
        got = dot(amp[...].reshape(bc * share, width), q[c]).astype(BF16)
        tall[c, :, pl.ds(pl.multiple_of(row * share, share), share), :] = got.reshape(bc, share, wide)

    def t_copy(c, source, slot, device):
        return pltpu.make_async_remote_copy(
            src_ref=piece(c, source), dst_ref=piece(c, source), send_sem=tsend.at[c, slot], recv_sem=trecv.at[c, source],
            device_id={"row": device}, device_id_type=MESH,
        )

    def t_direct(c):
        return [t_copy(c, row, k, lax.rem(row + k, ranks)) for k in hops] + [t_copy(c, row, 0, mate)]

    def t_forward(c):
        return [t_copy(c, lax.rem(row + ranks - k, ranks), k + 1, mate) for k in hops]

    pl.semaphore_wait(barrier, n + ranks // 2 - 1)

    @pl.loop(0, parts)
    def _(turn):
        for copy in t_direct(order(turn)):
            copy.start()

    p = partner_ref[...]
    local = lax.rem(p, n * rows)
    block = local // rows
    within = local - block * rows
    index = iota((1, rows), 1)
    key = jnp.where(block < me, within, index)
    same = iota((rows, rows), 0) == iota((rows, rows), 1)

    def column(line):
        return jnp.sum(jnp.where(same, line, 0.0), axis=1, keepdims=True)

    code = (block * rows + key).astype(F32)
    code_of = column(code)
    before = (code_of < code) & (code_of >= (block * rows).astype(F32))
    rank = jnp.sum(before.astype(F32), axis=0, keepdims=True).astype(I32)
    shift = lax.rem(block - me + n, n)
    owned = jnp.where(me < block, rank, 2 * half - 1 - rank) < half
    step = (shift - 1) * half + lax.rem(rank, half)
    place = jnp.where(block == me, rank, jnp.where(owned, 2 * half + step, own + step))
    places[me] = place

    def place_copy(d, source):
        return pltpu.make_async_remote_copy(
            src_ref=places.at[source], dst_ref=places.at[source], send_sem=gsend.at[d], recv_sem=grecv.at[source],
            device_id={"col": lax.rem(me + d, n)}, device_id_type=MESH,
        )

    for d in range(1, n):
        place_copy(d, me).start()

    tiles[slots] = jnp.zeros(tiles.shape[1:], BF16)

    @pl.loop(0, slots)
    def _(position):
        found = slots
        for s in range(slots):
            found = jnp.where((list_ref[s] == position) & (count_ref[0] > s), s, found)
        slot_s[position] = found

    for g in range(4):
        load_tiles(g).wait()
    for d in range(1, n):
        place_copy(d, lax.rem(me + d, n)).wait_recv()

    per = tile // rows

    @pl.loop(0, n)
    def _(o):
        hot_s[...] = one_hot_of(iota((rows, rows), 0) == places[o])
        part = pl.ds(pl.multiple_of(lax.rem(o, per) * rows, rows), rows)
        for c in range(bc):
            slot = slot_s[(o // per) * bc + c]
            got = dot(hot_s[...], tiles[slot, part, :]).astype(BF16)
            at = slice(c * tile, (c + 1) * tile)
            u_ref[o, :, at] = got[:own_p]
            for d in range(1, n):
                a = lax.rem(o + d, n)
                start = (n - d - 1) * half
                w_ref[a, start : start + half, at] = got[own + (d - 1) * half : own + d * half]

        @pl.when(o == n // 2)
        def _():
            for k in hops:
                t_copy(order(0), lax.rem(row + ranks - k, ranks), k, mate).wait_recv()
            for copy in t_forward(order(0)):
                copy.start()

    side = lax.rem(me, 2)
    pair = lax.rem(me // 2, 2)
    top = me // 4

    def route(c):
        swapped = jnp.where(c == parts - 1, 1, 0)
        first = side + swapped * (pair - side)
        second = pair + swapped * (side - pair)
        return first, second, 1 + swapped, 2 - swapped

    def turned(i):
        return lax.rem(top + 1 + i, m)

    def product(a, c, out):
        first = dot(u_ref[a], tall[c].reshape(depth, wide))
        out[: 2 * half, :] = first[: 2 * half]
        out[2 * half :, :] = first[2 * half :]
        out[2 * half : own, :] += dot(w_ref[a], t2[c])

    def remote(source, target, sent, arrived, device):
        return pltpu.make_async_remote_copy(
            src_ref=source, dst_ref=target, send_sem=sent, recv_sem=arrived,
            device_id={"col": device}, device_id_type=MESH,
        )

    def first_copy(c, k):
        first, _, weight, _ = route(c)
        device = me + weight * (1 - 2 * first)
        u = c * (n // 2) + k
        return (
            remote(q1s.at[u], q1r.at[u], q1a.at[u], q1b.at[u], device),
            remote(s1s.at[u], s1r.at[u], s1a.at[u], s1b.at[u], device),
        )

    def second_copy(c, i):
        _, second, _, weight = route(c)
        device = me + weight * (1 - 2 * second)
        u = c * m + i
        return (
            remote(q2s.at[u], q2r.at[u], q2a.at[u], q2b.at[u], device),
            remote(s2s.at[u], s2r.at[u], s2a.at[u], s2b.at[u], device),
        )

    def third_copy(c, i):
        device = me + 4 * (turned(i) - top)
        u = c * (m - 1) + i
        return (
            remote(q3s.at[u], q3r.at[u], q3a.at[u], q3b.at[u], device),
            remote(s3s.at[u], s3r.at[u], s3a.at[u], s3b.at[u], device),
        )

    def last_copy(c, d):
        device = lax.rem(me + d, n)
        u, v = c * n + d, c * n + n - d
        return (
            remote(xqs.at[u], xqr.at[v], xqa.at[u], xqb.at[v], device),
            remote(xss.at[u], xsr.at[v], xsa.at[u], xsb.at[v], device),
        )

    group = 128 // PIECE
    pieces = own_p // PIECE

    def here(count, k):
        return iota((count, 128), 1) == iota((count, 128), 0) + (k % group) * count

    def to_levels(part, k):
        most = jnp.max(jnp.abs(part), axis=1, keepdims=True)
        inverse = jnp.where(most > 1e-30, LEVELS / jnp.maximum(most, 1e-30), 0.0)
        scale = jnp.sum(jnp.where(here(part.shape[0], k), most * (1.0 / LEVELS), 0.0), axis=0, keepdims=True)
        return jnp.round(part * inverse).astype(I32).astype(I16), scale

    def from_levels(value, scale, k):
        return value.astype(I32).astype(F32) * jnp.sum(
            jnp.where(here(value.shape[0], k), scale, 0.0), axis=1, keepdims=True
        )

    def lines(k):
        return slice(k * PIECE, (k + 1) * PIECE)

    def pack(value, q_of, s_of):
        for g in range(0, pieces, group):
            line_of = None
            for k in range(g, min(g + group, pieces)):
                q_of[lines(k), :], scale = to_levels(value(k), k)
                line_of = scale if line_of is None else line_of + scale
            s_of[g // group : g // group + 1, :] = line_of

    def unpack(q_of, s_of, k):
        return from_levels(q_of[lines(k), :], s_of[k // group : k // group + 1, :], k)

    def start(copies):
        for copy in copies:
            copy.start()

    def arrive(copies):
        for copy in copies:
            copy.wait_recv()

    @pl.loop(0, parts)
    def _(turn):
        c = order(turn)

        @pl.when(turn < parts - 1)
        def _():
            later = order(turn + 1)
            for k in hops:
                t_copy(later, lax.rem(row + ranks - k, ranks), k, mate).wait_recv()
            for copy in t_forward(later):
                copy.start()

        t_copy(c, mate, 0, mate).wait_recv()
        for k in hops:
            t_copy(c, lax.rem(mate + ranks - k, ranks), k, mate).wait_recv()

        @pl.loop(0, bc)
        def _(k):
            at = pl.ds(pl.multiple_of(k * tile, tile), tile)
            t2[c, at, :] = dot(tall[c, k], mix[c]).astype(BF16)

        first, second, weight, other = route(c)

        @pl.loop(0, n // 2)
        def _(k):
            to = jnp.where(k < m, 1 - second, second)
            a = 4 * turned(lax.rem(k, m)) + weight * (1 - first) + other * to
            product(a, c, sbuf)
            pack(lambda j: sbuf[lines(j), :], q1s.at[c * (n // 2) + k], s1s.at[c * (n // 2) + k])
            start(first_copy(c, k))

    @pl.loop(0, parts + 4)
    def _(turn):
        @pl.when((turn >= 2) & (turn < parts + 2))
        def _():
            c = turn - 2
            first, second, weight, other = route(c)

            @pl.loop(0, m - 1)
            def _(i):
                product(4 * turned(i) + weight * first + other * second, c, sbuf)
                k = m + i
                arrive(first_copy(c, k))
                arrive(second_copy(c, i))
                u, v, x = c * (n // 2) + k, c * m + i, c * (m - 1) + i
                pack(
                    lambda j: sbuf[lines(j), :] + unpack(q1r.at[u], s1r.at[u], j) + unpack(q2r.at[v], s2r.at[v], j),
                    q3s.at[x], s3s.at[x],
                )
                start(third_copy(c, i))

        @pl.when(turn < parts)
        def _():
            c = order(turn)
            first, second, weight, other = route(c)

            @pl.loop(0, m)
            def _(i):
                product(4 * turned(i) + weight * first + other * (1 - second), c, sbuf)
                arrive(first_copy(c, i))
                u, v = c * (n // 2) + i, c * m + i
                pack(lambda j: sbuf[lines(j), :] + unpack(q1r.at[u], s1r.at[u], j), q2s.at[v], s2s.at[v])
                start(second_copy(c, i))

        @pl.when(turn == 2)
        def _():
            place_of = column(place.astype(F32))
            found = jnp.sum(
                jnp.where(iota((rows, rows), 0) == within, place_of, 0.0), axis=0, keepdims=True
            )
            mirror_of = column(jnp.where(block == me, rows + found, -1.0)).astype(I32)
            number = iota(hot.shape, 1)
            hot[...] = one_hot_of((number == place_of.astype(I32)) | (number == mirror_of))

        @pl.when((turn >= 3) & (turn < parts + 3))
        def _():
            c = turn - 3
            total = z.at[c]
            product(me, c, total)
            arrive(first_copy(c, 2 * m - 1))
            arrive(second_copy(c, m - 1))
            u, v = c * (n // 2) + 2 * m - 1, c * m + m - 1
            for i in range(m - 1):
                arrive(third_copy(c, i))
            for j in range(pieces):
                value = total[lines(j), :] + unpack(q1r.at[u], s1r.at[u], j) + unpack(q2r.at[v], s2r.at[v], j)
                for i in range(m - 1):
                    x = c * (m - 1) + i
                    value += unpack(q3r.at[x], s3r.at[x], j)
                total[lines(j), :] = value
            for d in range(1, n):
                xqs[c * n + d], xss[c * n + d] = to_levels(total[(d + 1) * half : (d + 2) * half, :], 0)
                start(last_copy(c, d))

        @pl.when(turn >= 4)
        def _():
            c = turn - 4

            def split(value, at, mixed):
                top_bits = value.astype(BF16)
                rest = (value - top_bits.astype(F32)).astype(BF16)
                for k, piece_of in ((0, top_bits), (1, rest)):
                    if mixed:
                        piece_of = dot(piece_of, mix[c]).astype(BF16)
                    stack[k, at, :] = piece_of

            split(z[c, :own, :], slice(0, own), False)
            split(z[c, : 2 * half, :], slice(rows, rows + 2 * half), True)
            for d in range(1, n):
                arrive(last_copy(c, d))
            far = jnp.concatenate([from_levels(xqr[c * n + v], xsr[c * n + v], 0) for v in range(1, n)], axis=0)
            split(far, slice(own, rows), True)
            chosen = dot(hot[...], stack[1]) + dot(hot[...], stack[0])
            top_bits = chosen.astype(BF16)
            rest = (chosen - top_bits.astype(F32)).astype(BF16)
            for k in range(0, width, wide):
                at = slice(k, k + wide)
                term = dot_nt(rest, q[c, at, :]) + dot_nt(top_bits, q[c, at, :])

                @pl.when(c == 0)
                def _():
                    out_ref[:, at] = term

                @pl.when(c > 0)
                def _():
                    out_ref[:, at] += term

    for d in range(1, n):
        place_copy(d, me).wait_send()

    @pl.loop(0, parts)
    def _(c):
        for copy in t_direct(c) + t_forward(c):
            copy.wait_send()
        for d in range(1, n):
            for copy in last_copy(c, d):
                copy.wait_send()

        @pl.loop(0, n // 2)
        def _(k):
            for copy in first_copy(c, k):
                copy.wait_send()

        @pl.loop(0, m)
        def _(i):
            for copy in second_copy(c, i):
                copy.wait_send()

        @pl.loop(0, m - 1)
        def _(i):
            for copy in third_copy(c, i):
                copy.wait_send()


def body(integrals, tile_count, tile_list, amplitudes, pair_energy, occ_energy, partner):
    n = lax.axis_size("col")
    ranks = lax.axis_size("row")
    rows = partner.shape[0]
    half = rows // n // 2
    own = (n + 1) * half
    own_p = -(-own // PIECE) * PIECE
    slots, tile = integrals.shape[2], integrals.shape[3]
    bc, share, width = amplitudes.shape
    occ = occ_energy.shape[0]
    depth = bc * tile
    parts = width // WIDE
    m = n // 4
    dma = pltpu.SemaphoreType.DMA
    lines = -(-own_p // 128)

    def packed(units):
        return [pltpu.VMEM((units, own_p, WIDE), I16), pltpu.VMEM((units, lines, 128), F32)] * 2

    def sems(units):
        return [dma((units,))] * 4

    counts = (parts * n // 2, parts * m, parts * (m - 1))
    anywhere = pl.BlockSpec(memory_space=pl.ANY)
    scalars = pl.BlockSpec(memory_space=pltpu.SMEM)
    vector = pl.BlockSpec(memory_space=pltpu.VMEM)
    total = pl.pallas_call(
        functools.partial(ladder_kernel, n, ranks, occ),
        out_shape=jax.ShapeDtypeStruct((rows, width), F32),
        in_specs=[scalars, scalars, vector, anywhere, anywhere],
        out_specs=vector,
        scratch_shapes=[
            pltpu.VMEM((slots + 1, tile, tile), BF16),
            pltpu.VMEM((bc, share, width), BF16),
            pltpu.VMEM((parts, bc, tile, WIDE), BF16),
            pltpu.VMEM((parts, depth, WIDE), BF16),
            pltpu.VMEM((n, own_p, depth), BF16),
            pltpu.VMEM((n, rows - own, depth), BF16),
            pltpu.VMEM((rows, rows), BF16),
            pltpu.VMEM((n, 1, rows), I32),
            pltpu.SMEM((slots,), I32),
            pltpu.VMEM((parts, width, WIDE), BF16),
            pltpu.VMEM((parts, WIDE, WIDE), BF16),
            pltpu.VMEM((own_p, WIDE), F32),
            pltpu.VMEM((parts, own_p, WIDE), F32),
            pltpu.VMEM((rows, rows + 2 * half), BF16),
            pltpu.VMEM((2, rows + 2 * half, WIDE), BF16),
            *packed(counts[0]), *packed(counts[1]), *packed(counts[2]),
            *([pltpu.VMEM((parts * n, half, WIDE), I16), pltpu.VMEM((parts * n, 1, 128), F32)] * 2),
            dma((4,)), dma, dma((parts, ranks)), dma((parts, ranks)), dma((n,)), dma((n,)),
            *sems(counts[0]), *sems(counts[1]), *sems(counts[2]), *sems(parts * n),
        ],
        compiler_params=pltpu.CompilerParams(
            collective_id=0, has_side_effects=True, vmem_limit_bytes=63 * 1024 * 1024
        ),
        name="ladder",
    )(tile_list.reshape(slots), tile_count.reshape(1), partner[None, :], integrals, amplitudes)
    pairs = (occ_energy[:, None] + occ_energy[None, :]).reshape(1, width)
    return total / (pair_energy[:, None] - pairs)


def solution(mesh):
    return jax.shard_map(
        body,
        mesh=mesh,
        in_specs=(
            P("row", "col", None, None, None),
            P("row", "col"),
            P("row", "col", None),
            P("col", "row", None),
            P(("row", "col")),
            P(),
            P(("row", "col")),
        ),
        out_specs=P(("row", "col"), None),
        check_vma=False,
    )
```

```python
import functools

import jax
import jax.numpy as jnp
from jax import lax
from jax.experimental import pallas as pl
from jax.experimental.pallas import tpu as pltpu
from jax.sharding import PartitionSpec as P

MESH = pl.DeviceIdType.MESH
F32, BF16, I32, I16 = jnp.float32, jnp.bfloat16, jnp.int32, jnp.int16
LEVELS = 32767.0
PIECE = 32
WIDE = 256


def schedule(parts, n):
    m = n // 4
    counts = {1: n // 2, 2: m, 3: m - 1}
    first, rest = slice(0, 1), slice(1, None)
    blocks = [(1, 0), (1, 1), (2, 1), (1, 2, first), (2, 0), (1, 2, rest), (3, 1), (1, 3), (3, 0), (2, 2), (0, 0), (4, 1), (3, 2)]
    blocks += [(2, 3), (4, 0), (5, 1), (3, 3), (4, 2), (5, 0), (4, 3), (5, 2), (5, 3)]
    if parts != 4:
        blocks = [(0, 0)] + [(kind, c) for kind in range(1, 6) for c in range(parts)]
    return [(kind, c, k) for kind, c, *some in blocks for k in list(range(counts.get(kind, 1)))[some[0] if some else slice(None)]]


def iota(shape, axis):
    return lax.broadcasted_iota(I32, shape, axis)


def one_hot_of(condition):
    return condition.astype(F32).astype(BF16)


def dot(a, b):
    return jnp.dot(a, b, preferred_element_type=F32)


def dot_nt(a, b):
    return lax.dot_general(a, b, (((1,), (1,)), ((), ())), preferred_element_type=F32)


def ladder_kernel(
    n, ranks, occ, list_ref, count_ref, partner_ref, integrals, amps, out_ref,
    tiles, amp, tall, t2, u_ref, w_ref, hot_u, hot_w, places, slot_s, q, mix, sbuf, z, hot_near, hot_far, near, chosen,
    qs, ss, qr, sr, xqs, xss, xqr, xsr,
    tile_sem, amp_sem, tsend, trecv, gsend, grecv, q_sent, s_sent, q_here, s_here, xq_sent, xs_sent, xq_here, xs_here,
):
    me = lax.axis_index("col")
    row = lax.axis_index("row")
    mate = row + 1 - 2 * lax.rem(row, 2)
    slots = list_ref.shape[0]
    rows = partner_ref.shape[1]
    half = rows // n // 2
    own = (n + 1) * half
    own_p = u_ref.shape[1]
    parts, bc, tile, wide = tall.shape
    depth = bc * tile
    share = amp.shape[1]
    width = amp.shape[2]
    groups = slots // 4
    m = n // 4
    hops = range(2, ranks, 2)

    def load_tiles(g):
        at = pl.ds(g * groups, groups)
        return pltpu.make_async_copy(integrals.at[0, 0, at], tiles.at[at], tile_sem.at[g])

    load_amp = pltpu.make_async_copy(amps, amp, amp_sem)
    load_amp.start()
    for g in range(4):
        load_tiles(g).start()

    barrier = pltpu.get_barrier_semaphore()
    for d in range(1, n):
        pl.semaphore_signal(barrier, inc=1, device_id={"col": lax.rem(me + d, n)}, device_id_type=MESH)
    pl.semaphore_signal(barrier, inc=1, device_id={"row": mate}, device_id_type=MESH)
    for k in hops:
        pl.semaphore_signal(barrier, inc=1, device_id={"row": lax.rem(row + k, ranks)}, device_id_type=MESH)

    def piece(c, source):
        return tall.at[c, :, pl.ds(pl.multiple_of(source * share, share), share), :]

    def t_copy(c, source, device):
        return pltpu.make_async_remote_copy(
            src_ref=piece(c, source), dst_ref=piece(c, source), send_sem=tsend, recv_sem=trecv.at[c, source],
            device_id={"row": device}, device_id_type=MESH,
        )

    def t_direct(c):
        return [t_copy(c, row, lax.rem(row + k, ranks)) for k in hops] + [t_copy(c, row, mate)]

    def t_forward(c):
        return [t_copy(c, lax.rem(row + ranks - k, ranks), mate) for k in hops]

    def reorder(c):
        number = iota((width, wide), 1) + c * wide
        i = number & (occ - 1)
        s = number // occ
        q[...] = one_hot_of(iota((width, wide), 0) == i * occ + ((s - i) & (occ - 1)))
        got = dot(amp[...].reshape(bc * share, width), q[...]).astype(BF16)
        tall[c, :, pl.ds(pl.multiple_of(row * share, share), share), :] = got.reshape(bc, share, wide)

    load_amp.wait()

    @pl.loop(0, parts)
    def _(turn):
        reorder(turn)

        @pl.when(turn == 0)
        def _():
            pl.semaphore_wait(barrier, n + ranks // 2 - 1)

        for copy in t_direct(turn):
            copy.start()

    p = partner_ref[...]
    local = lax.rem(p, n * rows)
    block = local // rows
    within = local - block * rows
    index = iota((1, rows), 1)
    key = jnp.where(block < me, within, index)
    same = iota((rows, rows), 0) == iota((rows, rows), 1)

    def column(line):
        return jnp.sum(jnp.where(same, line, 0.0), axis=1, keepdims=True)

    code = (block * rows + key).astype(F32)
    code_of = column(code)
    before = (code_of < code) & (code_of >= (block * rows).astype(F32))
    rank = jnp.sum(before.astype(F32), axis=0, keepdims=True).astype(I32)
    shift = lax.rem(block - me + n, n)
    owned = jnp.where(me < block, rank, 2 * half - 1 - rank) < half
    step = (shift - 1) * half + lax.rem(rank, half)
    place = jnp.where(block == me, rank, jnp.where(owned, 2 * half + step, own + step))
    places[me] = place

    def place_copy(d, source):
        return pltpu.make_async_remote_copy(
            src_ref=places.at[source], dst_ref=places.at[source], send_sem=gsend, recv_sem=grecv.at[source],
            device_id={"col": lax.rem(me + d, n)}, device_id_type=MESH,
        )

    for d in range(1, n):
        place_copy(d, me).start()

    tiles[slots] = jnp.zeros(tiles.shape[1:], BF16)

    @pl.loop(0, parts)
    def _(c):
        number = iota((wide, wide), 1)
        i = number & (occ - 1)
        s = number // occ + c * (wide // occ)
        mix[c] = one_hot_of(iota((wide, wide), 0) == number - i + ((s - i) & (occ - 1)))

    @pl.loop(0, slots)
    def _(position):
        found = slots
        for s in range(slots):
            found = jnp.where((list_ref[s] == position) & (count_ref[0] > s), s, found)
        slot_s[position] = found

    for g in range(4):
        load_tiles(g).wait()
    for d in range(1, n):
        place_copy(d, lax.rem(me + d, n)).wait_recv()

    per = tile // rows

    def sort(o, hot, first, store):
        hot[...] = one_hot_of(iota(hot.shape, 0) + first == places[o])
        part = pl.ds(pl.multiple_of(lax.rem(o, per) * rows, rows), rows)

        for c in range(bc):
            slot = slot_s[(o // per) * bc + c]
            store(dot(hot[...], tiles[slot, part, :]).astype(BF16), slice(c * tile, (c + 1) * tile))

    def sort_u(o):
        def store(got, at):
            u_ref[o, :, at] = got

        sort(o, hot_u, 0, store)

    @pl.loop(0, n)
    def _(o):
        def store(got, at):
            for d in range(1, n):
                a = lax.rem(o + d, n)
                start = (n - d - 1) * half
                w_ref[a, start : start + half, at] = got[(d - 1) * half : d * half]

        sort(o, hot_w, own, store)

        @pl.when(o == n // 2)
        def _():
            for k in hops:
                t_copy(0, lax.rem(row + ranks - k, ranks), mate).wait_recv()
            for copy in t_forward(0):
                copy.start()

    side = lax.rem(me, 2)
    pair = lax.rem(me // 2, 2)
    top = me // 4

    def route(c):
        swapped = jnp.where(c == 1, 1, 0)
        first = side + swapped * (pair - side)
        second = pair + swapped * (side - pair)
        return first, second, 1 + swapped, 2 - swapped

    def turned(i):
        return lax.rem(top + 1 + i, m)

    def product(a, c, out):
        first = dot(u_ref[a], tall[c].reshape(depth, wide))
        out[: 2 * half, :] = first[: 2 * half]
        out[2 * half :, :] = first[2 * half :]
        out[2 * half : own, :] += dot(w_ref[a], t2[c])

    def remote(source, target, sent, arrived, device):
        return pltpu.make_async_remote_copy(
            src_ref=source, dst_ref=target, send_sem=sent, recv_sem=arrived,
            device_id={"col": device}, device_id_type=MESH,
        )

    def unit_copies(u, device):
        return (
            remote(qs.at[u], qr.at[u], q_sent, q_here.at[u], device),
            remote(ss.at[u], sr.at[u], s_sent, s_here.at[u], device),
        )

    def last_copy(c, d):
        device = lax.rem(me + d, n)
        u, v = c * (n - 1) + d - 1, c * (n - 1) + n - d - 1
        return (
            remote(xqs.at[u], xqr.at[v], xq_sent, xq_here.at[c], device),
            remote(xss.at[u], xsr.at[v], xs_sent, xs_here.at[c], device),
        )

    def last_arrive(c):
        at = pl.ds(c * (n - 1), n - 1)
        device = lax.rem(me + 1, n)
        remote(xqs.at[at], xqr.at[at], xq_sent, xq_here.at[c], device).wait_recv()
        remote(xss.at[at], xsr.at[at], xs_sent, xs_here.at[c], device).wait_recv()

    group = 128 // PIECE
    pieces = own_p // PIECE

    def here(count, k):
        return iota((count, 128), 1) == iota((count, 128), 0) + (k % group) * count

    def to_levels(part, k):
        most = jnp.max(jnp.abs(part), axis=1, keepdims=True)
        inverse = jnp.where(most > 1e-30, LEVELS / jnp.maximum(most, 1e-30), 0.0)
        scale = jnp.sum(jnp.where(here(part.shape[0], k), most * (1.0 / LEVELS), 0.0), axis=0, keepdims=True)
        return jnp.round(part * inverse).astype(I32).astype(I16), scale

    def from_levels(value, scale, k):
        return value.astype(I32).astype(F32) * jnp.sum(
            jnp.where(here(value.shape[0], k), scale, 0.0), axis=1, keepdims=True
        )

    def lines(k):
        return slice(k * PIECE, (k + 1) * PIECE)

    def pack(u):
        for g in range(0, pieces, group):
            line_of = None
            for k in range(g, min(g + group, pieces)):
                qs[u, lines(k), :], scale = to_levels(sbuf[lines(k), :], k)
                line_of = scale if line_of is None else line_of + scale
            ss[u, g // group : g // group + 1, :] = line_of

    def add(u):
        for k in range(pieces):
            sbuf[lines(k), :] += from_levels(qr[u, lines(k), :], sr[u, k // group : k // group + 1, :], k)

    def start(copies):
        for copy in copies:
            copy.start()

    def arrive(copies):
        for copy in copies:
            copy.wait_recv()

    def amplitudes_of(c):
        @pl.when(c < parts - 1)
        def _():
            later = c + 1
            for k in hops:
                t_copy(later, lax.rem(row + ranks - k, ranks), mate).wait_recv()
            for copy in t_forward(later):
                copy.start()

        t_copy(c, mate, mate).wait_recv()
        for k in hops:
            t_copy(c, lax.rem(mate + ranks - k, ranks), mate).wait_recv()

        @pl.loop(0, bc)
        def _(k):
            at = pl.ds(pl.multiple_of(k * tile, tile), tile)
            t2[c, at, :] = dot(tall[c, k], mix[c]).astype(BF16)

    def unit(kind, c, k):
        def pick(*values):
            got = values[0]
            for at, value in enumerate(values[1:]):
                got = jnp.where(kind == at + 2, value, got)
            return got

        first, second, weight, other = route(c)
        on_first = pick(1 - first, first, first, first)
        on_second = pick(jnp.where(k < m, 1 - second, second), 1 - second, second, second)
        beside = jnp.where(kind == 4, m - 1, lax.rem(k, m))
        level = turned(beside)
        a = 4 * level + weight * on_first + other * on_second

        @pl.when((kind == 1) & (k == 0))
        def _():
            amplitudes_of(c)

        @pl.when((kind == 1) & ((c == 0) | ((c == 1) & (k >= m))))
        def _():
            sort_u(a)

        product(a, c, sbuf)
        base = c * (n - 1)

        @pl.loop(0, jnp.where(kind == 4, m + 1, kind - 1))
        def _(at):
            u = jnp.where(
                at == 0, pick(0, k, m + k, 2 * m - 1), jnp.where(at == 1, 2 * m + beside, 3 * m + at - 2)
            )
            arrive(unit_copies(base + u, me + 1 - 2 * side))
            add(base + u)

        @pl.when(kind < 4)
        def _():
            u = base + pick(k, 2 * m + k, 3 * m + k)
            pack(u)
            start(unit_copies(u, me + pick(weight * (1 - 2 * first), other * (1 - 2 * second), 4 * (level - top))))

        @pl.when((kind == 1) & (c == 1) & (k >= m))
        def _():
            sort_u(4 * level + side + 2 * pair)

        @pl.when(kind == 4)
        def _():
            z[c] = sbuf[...]
            for d in range(1, n):
                u = c * (n - 1) + d - 1
                xqs[u], xss[u] = to_levels(sbuf[(d + 1) * half : (d + 2) * half, :], 0)
                start(last_copy(c, d))

    def prepare():
        place_of = column(place.astype(F32))
        found = jnp.sum(jnp.where(iota((rows, rows), 0) == within, place_of, 0.0), axis=0, keepdims=True)
        mirror_of = column(jnp.where(block == me, rows + found, -1.0)).astype(I32)
        place_of = place_of.astype(I32)
        number = iota(hot_near.shape, 1)
        number = jnp.where(number < own, number, number + rows - own)
        hot_near[...] = one_hot_of((number == place_of) | (number == mirror_of))
        hot_far[...] = one_hot_of(iota(hot_far.shape, 1) + own == place_of)

    def halves(value):
        high = value.astype(BF16)
        return high, (value - high.astype(F32)).astype(BF16)

    def assemble(c):
        for k, half_of in enumerate(halves(z[c, :own, :])):
            near[k, :own, :] = half_of
        for k, half_of in enumerate(halves(z[c, : 2 * half, :])):
            near[k, own:, :] = dot(half_of, mix[c]).astype(BF16)
        chosen[...] = dot(hot_near[...], near[1]) + dot(hot_near[...], near[0])
        last_arrive(c)
        at = c * (n - 1)
        far = jnp.concatenate([from_levels(xqr[at + v], xsr[at + v], 0) for v in range(n - 1)], axis=0)
        high, low = [dot(half_of, mix[c]).astype(BF16) for half_of in halves(far)]
        out_ref[:, pl.ds(pl.multiple_of(c * wide, wide), wide)] = chosen[...] + (dot(hot_far[...], low) + dot(hot_far[...], high))

    table = [(kind * parts + turn) * n + k for kind, turn, k in schedule(parts, n)]

    @pl.loop(0, len(table))
    def _(step):
        entry = 0
        for at, value in enumerate(table):
            entry = jnp.where(step == at, value, entry)
        k = lax.rem(entry, n)
        turn = lax.rem(entry // n, parts)
        kind = entry // (n * parts)
        pl.when(kind == 0)(prepare)
        pl.when((kind > 0) & (kind < 5))(lambda: unit(kind, turn, k))
        pl.when(kind == 5)(lambda: assemble(turn))

    def sent(source, semaphore):
        pltpu.make_async_remote_copy(
            src_ref=source, dst_ref=source, send_sem=semaphore, recv_sem=amp_sem,
            device_id={"row": mate}, device_id_type=MESH,
        ).wait_send()

    sent(places.at[: n - 1], gsend)
    sent(tall.at[:, :, : share * (ranks - 1), :], tsend)
    for source, semaphore in ((qs, q_sent), (ss, s_sent), (xqs, xq_sent), (xss, xs_sent)):
        sent(source, semaphore)


def finish_kernel(occ, occ_ref, pair_ref, chosen_ref, out_ref, pieces, pair_of):
    rows, width = chosen_ref.shape
    wide = out_ref.shape[1]

    @pl.when(pl.program_id(0) == 0)
    def _():
        value = chosen_ref[...]
        high = value.astype(BF16)
        pieces[0] = high
        pieces[1] = (value - high.astype(F32)).astype(BF16)
        same = iota((rows, rows), 0) == iota((rows, rows), 1)
        pair_of[...] = jnp.broadcast_to(jnp.sum(jnp.where(same, pair_ref[...], 0.0), axis=1, keepdims=True), pair_of.shape)

    number = iota((1, wide), 1) + pl.program_id(0) * wide
    i, j = number // occ, number & (occ - 1)
    turned = one_hot_of(iota((width, wide), 0) == ((i + j) & (occ - 1)) * occ + i)
    first, second = jnp.zeros((1, wide), F32), jnp.zeros((1, wide), F32)
    for k in range(occ):
        first += jnp.where(i == k, occ_ref[k], 0.0)
        second += jnp.where(j == k, occ_ref[k], 0.0)
    total = dot(pieces[1], turned) + dot(pieces[0], turned)
    out_ref[...] = total / (pair_of[:, :1] - (first + second))


def body(integrals, tile_count, tile_list, amplitudes, pair_energy, occ_energy, partner):
    n = lax.axis_size("col")
    ranks = lax.axis_size("row")
    rows = partner.shape[0]
    half = rows // n // 2
    own = (n + 1) * half
    own_p = -(-own // PIECE) * PIECE
    slots, tile = integrals.shape[2], integrals.shape[3]
    bc, share, width = amplitudes.shape
    depth = bc * tile
    parts = width // WIDE
    occ = occ_energy.shape[0]
    dma = pltpu.SemaphoreType.DMA
    lines = -(-own_p // 128)

    units = parts * (n - 1)
    anywhere = pl.BlockSpec(memory_space=pl.ANY)
    scalars = pl.BlockSpec(memory_space=pltpu.SMEM)
    vector = pl.BlockSpec(memory_space=pltpu.VMEM)
    chosen = pl.pallas_call(
        functools.partial(ladder_kernel, n, ranks, occ),
        out_shape=jax.ShapeDtypeStruct((rows, width), F32),
        in_specs=[scalars, scalars, vector, anywhere, anywhere],
        out_specs=vector,
        scratch_shapes=[
            pltpu.VMEM((slots + 1, tile, tile), BF16),
            pltpu.VMEM((bc, share, width), BF16),
            pltpu.VMEM((parts, bc, tile, WIDE), BF16),
            pltpu.VMEM((parts, depth, WIDE), BF16),
            pltpu.VMEM((n, own_p, depth), BF16),
            pltpu.VMEM((n, rows - own, depth), BF16),
            pltpu.VMEM((own_p, rows), BF16),
            pltpu.VMEM((rows - own, rows), BF16),
            pltpu.VMEM((n, 1, rows), I32),
            pltpu.SMEM((slots,), I32),
            pltpu.VMEM((width, WIDE), BF16),
            pltpu.VMEM((parts, WIDE, WIDE), BF16),
            pltpu.VMEM((own_p, WIDE), F32),
            pltpu.VMEM((parts, own_p, WIDE), F32),
            pltpu.VMEM((rows, own + 2 * half), BF16),
            pltpu.VMEM((rows, rows - own), BF16),
            pltpu.VMEM((2, own + 2 * half, WIDE), BF16),
            pltpu.VMEM((rows, WIDE), F32),
            *([pltpu.VMEM((units, own_p, WIDE), I16), pltpu.VMEM((units, -(-own_p // 128), 128), F32)] * 2),
            *([pltpu.VMEM((units, half, WIDE), I16), pltpu.VMEM((units, 1, 128), F32)] * 2),
            dma((4,)), dma, dma, dma((parts, ranks)), dma, dma((n,)),
            dma, dma, dma((units,)), dma((units,)), dma, dma, dma((parts,)), dma((parts,)),
        ],
        compiler_params=pltpu.CompilerParams(
            collective_id=0, has_side_effects=True, vmem_limit_bytes=63 * 1024 * 1024
        ),
        name="ladder",
    )(tile_list.reshape(slots), tile_count.reshape(1), partner[None, :], integrals, amplitudes)

    whole = lambda k: (0, 0)
    return pl.pallas_call(
        functools.partial(finish_kernel, occ),
        grid=(parts,),
        in_specs=[scalars, pl.BlockSpec((1, rows), whole), pl.BlockSpec((rows, width), whole)],
        out_specs=pl.BlockSpec((rows, WIDE), lambda k: (0, k)),
        out_shape=jax.ShapeDtypeStruct((rows, width), F32),
        scratch_shapes=[pltpu.VMEM((2, rows, width), BF16), pltpu.VMEM((rows, 128), F32)],
        name="finish",
    )(occ_energy, pair_energy[None, :], chosen)


def solution(mesh):
    return jax.shard_map(
        body,
        mesh=mesh,
        in_specs=(
            P("row", "col", None, None, None),
            P("row", "col"),
            P("row", "col", None),
            P("col", "row", None),
            P(("row", "col")),
            P(),
            P(("row", "col")),
        ),
        out_specs=P(("row", "col"), None),
        check_vma=False,
    )
```

```python
import functools

import jax
import jax.numpy as jnp
from jax import lax
from jax.experimental import pallas as pl
from jax.experimental.pallas import tpu as pltpu
from jax.sharding import PartitionSpec as P

MESH = pl.DeviceIdType.MESH
F32, BF16, I32, I16 = jnp.float32, jnp.bfloat16, jnp.int32, jnp.int16
LEVELS = 32767.0
PIECE = 32
WIDE = 256


def schedule(parts, n):
    m = n // 4
    counts = {1: n // 2, 2: m, 3: m - 1}
    first, rest = slice(0, 1), slice(1, None)
    blocks = [(1, 0), (1, 1), (2, 1), (1, 2, first), (2, 0), (1, 2, rest), (3, 1), (1, 3), (3, 0), (2, 2), (0, 0), (4, 1), (3, 2)]
    blocks += [(4, 0), (2, 3), (5, 1), (3, 3), (4, 2), (5, 0), (4, 3), (5, 2), (5, 3)]
    if parts != 4:
        blocks = [(0, 0)] + [(kind, c) for kind in range(1, 6) for c in range(parts)]
    return [(kind, c, k) for kind, c, *some in blocks for k in list(range(counts.get(kind, 1)))[some[0] if some else slice(None)]]


def iota(shape, axis):
    return lax.broadcasted_iota(I32, shape, axis)


def one_hot_of(condition):
    return condition.astype(F32).astype(BF16)


def dot(a, b):
    return jnp.dot(a, b, preferred_element_type=F32)


def unsort(c, wide, width, occ):
    number = iota((1, width), 1)
    i, j = number // occ, number & (occ - 1)
    return one_hot_of(iota((wide, width), 0) + c * wide == ((i + j) & (occ - 1)) * occ + i)


def ladder_kernel(
    n, ranks, occ, list_ref, count_ref, partner_ref, integrals, amps, out_ref, last_ref,
    tiles, amp, tall, t2, u_ref, w_ref, hot_u, hot_w, places, slot_s, q, mix, sbuf, z, hot_near, hot_far, near, chosen, turned_q,
    qs, ss, qr, sr, xqs, xss, xqr, xsr,
    tile_sem, amp_sem, tsend, trecv, gsend, grecv, q_sent, s_sent, q_here, s_here, xq_sent, xs_sent, xq_here, xs_here,
):
    me = lax.axis_index("col")
    row = lax.axis_index("row")
    mate = row + 1 - 2 * lax.rem(row, 2)
    slots = list_ref.shape[0]
    rows = partner_ref.shape[1]
    half = rows // n // 2
    own = (n + 1) * half
    own_p = u_ref.shape[1]
    parts, bc, tile, wide = tall.shape
    depth = bc * tile
    share = amp.shape[1]
    width = amp.shape[2]
    groups = slots // 4
    m = n // 4
    hops = range(2, ranks, 2)

    def load_tiles(g):
        at = pl.ds(g * groups, groups)
        return pltpu.make_async_copy(integrals.at[0, 0, at], tiles.at[at], tile_sem.at[g])

    load_amp = pltpu.make_async_copy(amps, amp, amp_sem)
    load_amp.start()
    for g in range(4):
        load_tiles(g).start()

    barrier = pltpu.get_barrier_semaphore()
    for d in range(1, n):
        pl.semaphore_signal(barrier, inc=1, device_id={"col": lax.rem(me + d, n)}, device_id_type=MESH)
    pl.semaphore_signal(barrier, inc=1, device_id={"row": mate}, device_id_type=MESH)
    for k in hops:
        pl.semaphore_signal(barrier, inc=1, device_id={"row": lax.rem(row + k, ranks)}, device_id_type=MESH)

    def piece(c, source):
        return tall.at[c, :, pl.ds(pl.multiple_of(source * share, share), share), :]

    def t_copy(c, source, device):
        return pltpu.make_async_remote_copy(
            src_ref=piece(c, source), dst_ref=piece(c, source), send_sem=tsend, recv_sem=trecv.at[c, source],
            device_id={"row": device}, device_id_type=MESH,
        )

    def t_direct(c):
        return [t_copy(c, row, lax.rem(row + k, ranks)) for k in hops] + [t_copy(c, row, mate)]

    def t_forward(c):
        return [t_copy(c, lax.rem(row + ranks - k, ranks), mate) for k in hops]

    def reorder(c):
        number = iota((width, wide), 1) + c * wide
        i = number & (occ - 1)
        s = number // occ
        q[...] = one_hot_of(iota((width, wide), 0) == i * occ + ((s - i) & (occ - 1)))
        got = dot(amp[...].reshape(bc * share, width), q[...]).astype(BF16)
        tall[c, :, pl.ds(pl.multiple_of(row * share, share), share), :] = got.reshape(bc, share, wide)

    load_amp.wait()

    @pl.loop(0, parts)
    def _(turn):
        reorder(turn)

        @pl.when(turn == 0)
        def _():
            pl.semaphore_wait(barrier, n + ranks // 2 - 1)

        for copy in t_direct(turn):
            copy.start()

    p = partner_ref[...]
    local = lax.rem(p, n * rows)
    block = local // rows
    within = local - block * rows
    index = iota((1, rows), 1)
    key = jnp.where(block < me, within, index)
    same = iota((rows, rows), 0) == iota((rows, rows), 1)

    def column(line):
        return jnp.sum(jnp.where(same, line, 0.0), axis=1, keepdims=True)

    code = (block * rows + key).astype(F32)
    code_of = column(code)
    before = (code_of < code) & (code_of >= (block * rows).astype(F32))
    rank = jnp.sum(before.astype(F32), axis=0, keepdims=True).astype(I32)
    shift = lax.rem(block - me + n, n)
    owned = jnp.where(me < block, rank, 2 * half - 1 - rank) < half
    step = (shift - 1) * half + lax.rem(rank, half)
    place = jnp.where(block == me, rank, jnp.where(owned, 2 * half + step, own + step))
    places[me] = place

    def place_copy(d, source):
        return pltpu.make_async_remote_copy(
            src_ref=places.at[source], dst_ref=places.at[source], send_sem=gsend, recv_sem=grecv.at[source],
            device_id={"col": lax.rem(me + d, n)}, device_id_type=MESH,
        )

    for d in range(1, n):
        place_copy(d, me).start()

    tiles[slots] = jnp.zeros(tiles.shape[1:], BF16)

    @pl.loop(0, parts)
    def _(c):
        number = iota((wide, wide), 1)
        i = number & (occ - 1)
        s = number // occ + c * (wide // occ)
        mix[c] = one_hot_of(iota((wide, wide), 0) == number - i + ((s - i) & (occ - 1)))

    @pl.loop(0, slots)
    def _(position):
        found = slots
        for s in range(slots):
            found = jnp.where((list_ref[s] == position) & (count_ref[0] > s), s, found)
        slot_s[position] = found

    for g in range(4):
        load_tiles(g).wait()
    for d in range(1, n):
        place_copy(d, lax.rem(me + d, n)).wait_recv()

    per = tile // rows

    def sort(o, hot, first, store):
        hot[...] = one_hot_of(iota(hot.shape, 0) + first == places[o])
        part = pl.ds(pl.multiple_of(lax.rem(o, per) * rows, rows), rows)

        for c in range(bc):
            slot = slot_s[(o // per) * bc + c]
            store(dot(hot[...], tiles[slot, part, :]).astype(BF16), slice(c * tile, (c + 1) * tile))

    def sort_u(o):
        def store(got, at):
            u_ref[o, :, at] = got

        sort(o, hot_u, 0, store)

    @pl.loop(0, n)
    def _(o):
        def store(got, at):
            for d in range(1, n):
                a = lax.rem(o + d, n)
                start = (n - d - 1) * half
                w_ref[a, start : start + half, at] = got[(d - 1) * half : d * half]

        sort(o, hot_w, own, store)

        @pl.when(o == n // 2)
        def _():
            for k in hops:
                t_copy(0, lax.rem(row + ranks - k, ranks), mate).wait_recv()
            for copy in t_forward(0):
                copy.start()

    side = lax.rem(me, 2)
    pair = lax.rem(me // 2, 2)
    top = me // 4

    def route(c):
        swapped = jnp.where(c == 1, 1, 0)
        first = side + swapped * (pair - side)
        second = pair + swapped * (side - pair)
        return first, second, 1 + swapped, 2 - swapped

    def turned(i):
        return lax.rem(top + 1 + i, m)

    def product(a, c, out):
        first = dot(u_ref[a], tall[c].reshape(depth, wide))
        out[: 2 * half, :] = first[: 2 * half]
        out[2 * half :, :] = first[2 * half :]
        out[2 * half : own, :] += dot(w_ref[a], t2[c])

    def remote(source, target, sent, arrived, device):
        return pltpu.make_async_remote_copy(
            src_ref=source, dst_ref=target, send_sem=sent, recv_sem=arrived,
            device_id={"col": device}, device_id_type=MESH,
        )

    def unit_copies(u, device):
        return (
            remote(qs.at[u], qr.at[u], q_sent, q_here.at[u], device),
            remote(ss.at[u], sr.at[u], s_sent, s_here.at[u], device),
        )

    def last_copy(c, d):
        device = lax.rem(me + d, n)
        u, v = c * (n - 1) + d - 1, c * (n - 1) + n - d - 1
        return (
            remote(xqs.at[u], xqr.at[v], xq_sent, xq_here.at[c], device),
            remote(xss.at[u], xsr.at[v], xs_sent, xs_here.at[c], device),
        )

    def last_arrive(c):
        at = pl.ds(c * (n - 1), n - 1)
        device = lax.rem(me + 1, n)
        remote(xqs.at[at], xqr.at[at], xq_sent, xq_here.at[c], device).wait_recv()
        remote(xss.at[at], xsr.at[at], xs_sent, xs_here.at[c], device).wait_recv()

    group = 128 // PIECE
    pieces = own_p // PIECE

    def here(count, k):
        return iota((count, 128), 1) == iota((count, 128), 0) + (k % group) * count

    def to_levels(part, k):
        most = jnp.max(jnp.abs(part), axis=1, keepdims=True)
        inverse = jnp.where(most > 1e-30, LEVELS / jnp.maximum(most, 1e-30), 0.0)
        scale = jnp.sum(jnp.where(here(part.shape[0], k), most * (1.0 / LEVELS), 0.0), axis=0, keepdims=True)
        return jnp.round(part * inverse).astype(I32).astype(I16), scale

    def from_levels(value, scale, k):
        return value.astype(I32).astype(F32) * jnp.sum(
            jnp.where(here(value.shape[0], k), scale, 0.0), axis=1, keepdims=True
        )

    def lines(k):
        return slice(k * PIECE, (k + 1) * PIECE)

    def pack(u):
        for g in range(0, pieces, group):
            line_of = None
            for k in range(g, min(g + group, pieces)):
                qs[u, lines(k), :], scale = to_levels(sbuf[lines(k), :], k)
                line_of = scale if line_of is None else line_of + scale
            ss[u, g // group : g // group + 1, :] = line_of

    def add(u):
        for k in range(pieces):
            sbuf[lines(k), :] += from_levels(qr[u, lines(k), :], sr[u, k // group : k // group + 1, :], k)

    def start(copies):
        for copy in copies:
            copy.start()

    def arrive(copies):
        for copy in copies:
            copy.wait_recv()

    def amplitudes_of(c):
        @pl.when(c < parts - 1)
        def _():
            later = c + 1
            for k in hops:
                t_copy(later, lax.rem(row + ranks - k, ranks), mate).wait_recv()
            for copy in t_forward(later):
                copy.start()

        t_copy(c, mate, mate).wait_recv()
        for k in hops:
            t_copy(c, lax.rem(mate + ranks - k, ranks), mate).wait_recv()

        @pl.loop(0, bc)
        def _(k):
            at = pl.ds(pl.multiple_of(k * tile, tile), tile)
            t2[c, at, :] = dot(tall[c, k], mix[c]).astype(BF16)

    def unit(kind, c, k):
        def pick(*values):
            got = values[0]
            for at, value in enumerate(values[1:]):
                got = jnp.where(kind == at + 2, value, got)
            return got

        first, second, weight, other = route(c)
        on_first = pick(1 - first, first, first, first)
        on_second = pick(jnp.where(k < m, 1 - second, second), 1 - second, second, second)
        beside = jnp.where(kind == 4, m - 1, lax.rem(k, m))
        level = turned(beside)
        a = 4 * level + weight * on_first + other * on_second

        @pl.when((kind == 1) & (k == 0))
        def _():
            amplitudes_of(c)

        @pl.when((kind == 1) & ((c == 0) | ((c == 1) & (k >= m))))
        def _():
            sort_u(a)

        product(a, c, sbuf)
        base = c * (n - 1)

        @pl.loop(0, jnp.where(kind == 4, m + 1, kind - 1))
        def _(at):
            u = jnp.where(
                at == 0, pick(0, k, m + k, 2 * m - 1), jnp.where(at == 1, 2 * m + beside, 3 * m + at - 2)
            )
            arrive(unit_copies(base + u, me + 1 - 2 * side))
            add(base + u)

        @pl.when(kind < 4)
        def _():
            u = base + pick(k, 2 * m + k, 3 * m + k)
            pack(u)
            start(unit_copies(u, me + pick(weight * (1 - 2 * first), other * (1 - 2 * second), 4 * (level - top))))

        @pl.when((kind == 1) & (c == 1) & (k >= m))
        def _():
            sort_u(4 * level + side + 2 * pair)

        @pl.when(kind == 4)
        def _():
            z[c] = sbuf[...]
            for d in range(1, n):
                u = c * (n - 1) + d - 1
                xqs[u], xss[u] = to_levels(sbuf[(d + 1) * half : (d + 2) * half, :], 0)
                start(last_copy(c, d))

    def prepare():
        place_of = column(place.astype(F32))
        found = jnp.sum(jnp.where(iota((rows, rows), 0) == within, place_of, 0.0), axis=0, keepdims=True)
        mirror_of = column(jnp.where(block == me, rows + found, -1.0)).astype(I32)
        place_of = place_of.astype(I32)
        number = iota(hot_near.shape, 1)
        number = jnp.where(number < own, number, number + rows - own)
        hot_near[...] = one_hot_of((number == place_of) | (number == mirror_of))
        hot_far[...] = one_hot_of(iota(hot_far.shape, 1) + own == place_of)
        out_ref[...] = jnp.zeros(out_ref.shape, F32)

        @pl.loop(0, parts - 1)
        def _(c):
            turned_q[c] = unsort(c, wide, width, occ)

    def halves(value):
        high = value.astype(BF16)
        return high, (value - high.astype(F32)).astype(BF16)

    def assemble(c):
        for k, half_of in enumerate(halves(z[c, :own, :])):
            near[k, :own, :] = half_of
        for k, half_of in enumerate(halves(z[c, : 2 * half, :])):
            near[k, own:, :] = dot(half_of, mix[c]).astype(BF16)
        chosen[...] = dot(hot_near[...], near[1]) + dot(hot_near[...], near[0])
        last_arrive(c)
        at = c * (n - 1)
        far = jnp.concatenate([from_levels(xqr[at + v], xsr[at + v], 0) for v in range(n - 1)], axis=0)
        high, low = [dot(half_of, mix[c]).astype(BF16) for half_of in halves(far)]
        chosen[...] += dot(hot_far[...], low) + dot(hot_far[...], high)

        @pl.when(c == parts - 1)
        def _():
            last_ref[...] = chosen[...]

        @pl.when(c < parts - 1)
        def _():
            high, low = halves(chosen[...])
            for k in range(0, width, wide):
                at = slice(k, k + wide)
                out_ref[:, at] += dot(low, turned_q[c, :, at]) + dot(high, turned_q[c, :, at])

    table = [(kind * parts + turn) * n + k for kind, turn, k in schedule(parts, n)]

    @pl.loop(0, len(table))
    def _(step):
        entry = 0
        for at, value in enumerate(table):
            entry = jnp.where(step == at, value, entry)
        k = lax.rem(entry, n)
        turn = lax.rem(entry // n, parts)
        kind = entry // (n * parts)
        pl.when(kind == 0)(prepare)
        pl.when((kind > 0) & (kind < 5))(lambda: unit(kind, turn, k))
        pl.when(kind == 5)(lambda: assemble(turn))

    def sent(source, semaphore):
        pltpu.make_async_remote_copy(
            src_ref=source, dst_ref=source, send_sem=semaphore, recv_sem=amp_sem,
            device_id={"row": mate}, device_id_type=MESH,
        ).wait_send()

    sent(places.at[: n - 1], gsend)
    sent(tall.at[:, :, : share * (ranks - 1), :], tsend)
    for source, semaphore in ((qs, q_sent), (ss, s_sent), (xqs, xq_sent), (xss, xs_sent)):
        sent(source, semaphore)


def finish_kernel(occ, occ_ref, pair_ref, sum_ref, last_ref, out_ref, turned_q, energy):
    lines, width = sum_ref.shape
    wide = last_ref.shape[1]

    @pl.when(pl.program_id(0) == 0)
    def _():
        turned_q[...] = unsort(width // wide - 1, wide, width, occ)
        number = iota((1, width), 1)
        i, j = number // occ, number & (occ - 1)
        first, second = jnp.zeros((1, width), F32), jnp.zeros((1, width), F32)
        for k in range(occ):
            first += jnp.where(i == k, occ_ref[k], 0.0)
            second += jnp.where(j == k, occ_ref[k], 0.0)
        energy[...] = first + second

    value = last_ref[...]
    high = value.astype(BF16)
    low = (value - high.astype(F32)).astype(BF16)
    same = iota((lines, lines), 0) == iota((lines, lines), 1)
    pair_of = jnp.sum(jnp.where(same, pair_ref[...], 0.0), axis=1, keepdims=True)
    total = sum_ref[...] + (dot(low, turned_q[...]) + dot(high, turned_q[...]))
    out_ref[...] = total / (pair_of - energy[...])


def body(integrals, tile_count, tile_list, amplitudes, pair_energy, occ_energy, partner):
    n = lax.axis_size("col")
    ranks = lax.axis_size("row")
    rows = partner.shape[0]
    half = rows // n // 2
    own = (n + 1) * half
    own_p = -(-own // PIECE) * PIECE
    slots, tile = integrals.shape[2], integrals.shape[3]
    bc, share, width = amplitudes.shape
    depth = bc * tile
    parts = width // WIDE
    occ = occ_energy.shape[0]
    dma = pltpu.SemaphoreType.DMA
    lines = -(-own_p // 128)

    units = parts * (n - 1)
    anywhere = pl.BlockSpec(memory_space=pl.ANY)
    scalars = pl.BlockSpec(memory_space=pltpu.SMEM)
    vector = pl.BlockSpec(memory_space=pltpu.VMEM)
    total, last = pl.pallas_call(
        functools.partial(ladder_kernel, n, ranks, occ),
        out_shape=[jax.ShapeDtypeStruct((rows, width), F32), jax.ShapeDtypeStruct((rows, WIDE), F32)],
        in_specs=[scalars, scalars, vector, anywhere, anywhere],
        out_specs=[vector, vector],
        scratch_shapes=[
            pltpu.VMEM((slots + 1, tile, tile), BF16),
            pltpu.VMEM((bc, share, width), BF16),
            pltpu.VMEM((parts, bc, tile, WIDE), BF16),
            pltpu.VMEM((parts, depth, WIDE), BF16),
            pltpu.VMEM((n, own_p, depth), BF16),
            pltpu.VMEM((n, rows - own, depth), BF16),
            pltpu.VMEM((own_p, rows), BF16),
            pltpu.VMEM((rows - own, rows), BF16),
            pltpu.VMEM((n, 1, rows), I32),
            pltpu.SMEM((slots,), I32),
            pltpu.VMEM((width, WIDE), BF16),
            pltpu.VMEM((parts, WIDE, WIDE), BF16),
            pltpu.VMEM((own_p, WIDE), F32),
            pltpu.VMEM((parts, own_p, WIDE), F32),
            pltpu.VMEM((rows, own + 2 * half), BF16),
            pltpu.VMEM((rows, rows - own), BF16),
            pltpu.VMEM((2, own + 2 * half, WIDE), BF16),
            pltpu.VMEM((rows, WIDE), F32),
            pltpu.VMEM((parts - 1, WIDE, width), BF16),
            *([pltpu.VMEM((units, own_p, WIDE), I16), pltpu.VMEM((units, -(-own_p // 128), 128), F32)] * 2),
            *([pltpu.VMEM((units, half, WIDE), I16), pltpu.VMEM((units, 1, 128), F32)] * 2),
            dma((4,)), dma, dma, dma((parts, ranks)), dma, dma((n,)),
            dma, dma, dma((units,)), dma((units,)), dma, dma, dma((parts,)), dma((parts,)),
        ],
        compiler_params=pltpu.CompilerParams(
            collective_id=0, has_side_effects=True, vmem_limit_bytes=63 * 1024 * 1024
        ),
        name="ladder",
    )(tile_list.reshape(slots), tile_count.reshape(1), partner[None, :], integrals, amplitudes)

    lines = max(rows // 4, 128)
    return pl.pallas_call(
        functools.partial(finish_kernel, occ),
        grid=(rows // lines,),
        in_specs=[
            scalars,
            pl.BlockSpec((1, lines), lambda k: (0, k)),
            pl.BlockSpec((lines, width), lambda k: (k, 0)),
            pl.BlockSpec((lines, WIDE), lambda k: (k, 0)),
        ],
        out_specs=pl.BlockSpec((lines, width), lambda k: (k, 0)),
        out_shape=jax.ShapeDtypeStruct((rows, width), F32),
        scratch_shapes=[pltpu.VMEM((WIDE, width), BF16), pltpu.VMEM((1, width), F32)],
        name="finish",
    )(occ_energy, pair_energy[None, :], total, last)


def solution(mesh):
    return jax.shard_map(
        body,
        mesh=mesh,
        in_specs=(
            P("row", "col", None, None, None),
            P("row", "col"),
            P("row", "col", None),
            P("col", "row", None),
            P(("row", "col")),
            P(),
            P(("row", "col")),
        ),
        out_specs=P(("row", "col"), None),
        check_vma=False,
    )
```
